32 devices in a mesh: dp: 4 (over y, x), ctx: 8 (over z, core).
Axes of the slice: x: 2, y: 2, z: 4, core: 2. Of those that a mesh axis runs over, the one named last changes fastest.
Arguments:
- inputs: bfloat16 [4, 1024, 4096], P('dp', 'ctx'), may hold values from -8 to 8
- queries: bfloat16 [4, 1024, 8192], P('dp', 'ctx'), may hold values from -256 to 256
- grad_output: bfloat16 [4, 1024, 8192], P('dp', 'ctx'), may hold values from -6 to 6
- kv_weight: bfloat16 [4096, 1024], P(('dp', 'ctx')), may hold values from -1 to 1
Outputs:
- attn_out: bfloat16 [4, 1024, 8192], P('dp', 'ctx')
- grad_query: bfloat16 [4, 1024, 8192], P('dp', 'ctx')
- grad_inputs: bfloat16 [4, 1024, 4096], P('dp', 'ctx')
- grad_weight: float32 [4096, 1024], P(('dp', 'ctx'))
The draws below stay inside these ranges and needn't reach their ends.
All inputs are finite; a program needn't handle non-finite values.
Results may differ from the reference program's by a relative error of at most 0.035.
Values may be sent and summed in bfloat16 or wider, within the bound.
No kernel may reach another device: no remote copies, remote signals or barrier semaphores. Data moves between devices by JAX's collectives and lax.ppermute only.
A program may use at most 128 MiB of HBM per device.

```python
import jax
import jax.numpy as jnp
from jax import lax

D = 4096
HQ = 64
KVH = 4
DH = 128
SEQLEN = 1024
SEQS = 4


def input_field(key):
    normal_key = jax.random.fold_in(key, 101)
    field = jax.random.normal(normal_key, (SEQS, SEQLEN, D), jnp.float32)
    return jnp.clip(field, -8.0, 8.0)


def weight_field(key):
    normal_key = jax.random.fold_in(key, 201)
    field = jax.random.normal(normal_key, (D, 2 * KVH * DH), jnp.float32)
    return jnp.clip(field, -2.5, 2.5) * D ** (-0.5)


def draw_inputs(key, part):
    return input_field(key).astype(jnp.bfloat16)


def draw_kv_weight(key, part):
    return weight_field(key).astype(jnp.bfloat16)


def draw_queries(key, part):
    base_key = jax.random.fold_in(key, 301)
    field = jnp.clip(jax.random.normal(base_key, (SEQS, SEQLEN, HQ * DH), jnp.float32), -6.0, 6.0)
    return field.astype(jnp.bfloat16)


def shard_levels(own_key, dims, cuts, low, top_value):
    def one(position, shards_of):
        draws = jax.random.uniform(jax.random.fold_in(jax.random.fold_in(own_key, 6), position), (shards_of,), jnp.float32, low / len(cuts), top_value / len(cuts))
        return jnp.repeat(jnp.exp(draws), dims[position] // shards_of).reshape((-1,) + (1,) * (len(dims) - position - 1))

    loudness = one(*cuts[0])
    for cut in cuts[1:]:
        loudness = loudness * one(*cut)
    return loudness


def gaussian(rng, shape, spread, most, split=(), kind=jnp.bfloat16):
    values = jax.random.normal(rng, shape, jnp.float32) * spread
    if len(split) > 0:
        values = shard_levels(rng, shape, split, -0.22, 0.18) * values
    return jnp.clip(values, min=-most, max=most).astype(kind)


def setup_inputs(seed: int = 0) -> dict:
    splits = jax.random.split(jax.random.key(seed), 5)
    inputs = draw_inputs(jax.random.fold_in(splits[4], 71), 0)
    queries = draw_queries(jax.random.fold_in(splits[4], 71), 0)
    grad_output = gaussian(splits[2], (SEQS, SEQLEN, HQ * DH), 1.0, 6.0, ((0, 4), (1, 8)))
    kv_weight = draw_kv_weight(jax.random.fold_in(splits[4], 71), 0)
    return dict(inputs=inputs, queries=queries, grad_output=grad_output, kv_weight=kv_weight)


ROPE_BASE = 500000.0


def rope_tables(positions, head_dim):
    half_dim = head_dim // 2
    frequency = ROPE_BASE ** (-2.0 * jnp.arange(half_dim, dtype=jnp.float32) / head_dim)
    angles = positions.astype(jnp.float32)[:, None] * frequency[None, :]
    return jnp.cos(angles)[:, None, :], jnp.sin(angles)[:, None, :]


def rotary(values, positions):
    half_dim = values.shape[-1] // 2
    cosine, sine_table = rope_tables(positions, values.shape[-1])
    first_half = values[..., :half_dim]
    second = values[..., half_dim:]
    return jnp.concatenate([first_half * cosine - second * sine_table, second * cosine + first_half * sine_table], axis=-1)


def rotary_back(gradient, positions):
    half_dim = gradient.shape[-1] // 2
    cosine, sine_table = rope_tables(positions, gradient.shape[-1])
    first_half = gradient[..., :half_dim]
    second = gradient[..., half_dim:]
    return jnp.concatenate([first_half * cosine + second * sine_table, second * cosine - first_half * sine_table], axis=-1)


def rounded(operand):
    return lax.optimization_barrier(operand.astype(jnp.bfloat16)).astype(jnp.float32)


def one_sequence(inputs_seq, query_seq, grad_seq, kv_weight):
    length = inputs_seq.shape[0]
    half_cols = KVH * DH
    group_size = HQ // KVH
    projected = jnp.dot(inputs_seq, kv_weight, preferred_element_type=jnp.float32)
    positions = jnp.arange(length, dtype=jnp.int32)
    key_rows = rotary(projected[:, :half_cols].reshape(length, KVH, DH), positions).astype(jnp.bfloat16)
    value_rows = projected[:, half_cols:].reshape(length, KVH, DH).astype(jnp.bfloat16)
    queries = query_seq.reshape(length, KVH, group_size, DH).astype(jnp.float32)
    cotangent = grad_seq.reshape(length, KVH, group_size, DH).astype(jnp.float32)
    causal = positions[:, None] >= positions[None, :]
    score_scale = DH ** -0.5
    outs_heads = []
    grad_q_heads = []
    grad_k_heads = []
    grad_v_heads = []
    for head_index in range(KVH):
        query_head = queries[:, head_index]
        key_head = key_rows[:, head_index].astype(jnp.float32)
        value_head = value_rows[:, head_index].astype(jnp.float32)
        grad_head = cotangent[:, head_index]
        scores = jnp.einsum("qgd,kd->gqk", query_head, key_head) * score_scale
        scores = jnp.where(causal[None], scores, -jnp.inf)
        row_top = jnp.max(scores, axis=-1, keepdims=True)
        weights = jnp.exp(scores - row_top)
        row_total = jnp.sum(weights, axis=-1, keepdims=True)
        weighted = jnp.einsum("gqk,kd->gqd", rounded(weights), value_head) / row_total
        attn_rounded = lax.optimization_barrier(jnp.transpose(weighted, (1, 0, 2)).astype(jnp.bfloat16))
        log_total = row_top + jnp.log(row_total)
        row_delta = jnp.sum(grad_head * attn_rounded.astype(jnp.float32), axis=-1)
        probs_now = jnp.exp(scores - log_total)
        dprobs = jnp.einsum("qgd,kd->gqk", grad_head, value_head)
        dscores = probs_now * (dprobs - jnp.transpose(row_delta)[:, :, None])
        dscores_b = rounded(dscores)
        grad_q_heads.append((jnp.einsum("gqk,kd->qgd", dscores_b, key_head) * score_scale).astype(jnp.bfloat16))
        grad_k_heads.append(jnp.einsum("gqk,qgd->kd", dscores_b, query_head) * score_scale)
        grad_v_heads.append(jnp.einsum("gqk,qgd->kd", rounded(probs_now), grad_head))
        outs_heads.append(attn_rounded)
    attn_out = jnp.stack(outs_heads, axis=1).reshape(length, HQ * DH)
    grad_query = jnp.stack(grad_q_heads, axis=1).reshape(length, HQ * DH)
    grad_keys = jnp.stack(grad_k_heads, axis=1)
    grad_values = jnp.stack(grad_v_heads, axis=1)
    grad_projected = jnp.concatenate([rotary_back(grad_keys, positions).reshape(length, half_cols), grad_values.reshape(length, half_cols)], axis=1).astype(jnp.bfloat16)
    grad_inputs = jnp.dot(grad_projected, kv_weight.T, preferred_element_type=jnp.float32).astype(jnp.bfloat16)
    grad_weight = jnp.dot(inputs_seq.T, grad_projected, preferred_element_type=jnp.float32)
    return attn_out, grad_query, grad_inputs, grad_weight


def reference(inputs, queries, grad_output, kv_weight):
    def per_sequence(operands):
        return one_sequence(operands[0], operands[1], operands[2], kv_weight)

    attn_out, grad_query, grad_inputs, grad_parts = lax.map(per_sequence, (inputs, queries, grad_output))
    return attn_out, grad_query, grad_inputs, jnp.sum(grad_parts, axis=0)
```

```python
import functools
import math

import jax
import jax.numpy as jnp
from jax import lax
from jax.experimental import pallas as pl
from jax.experimental.pallas import tpu as pltpu
from jax.sharding import PartitionSpec as P

DH = 128
ROPE_BASE = 500000.0
F32 = jnp.float32
BF16 = jnp.bfloat16
CHUNKS = 2


def dot(a, b, ca, cb):
    return lax.dot_general(a, b, (((ca,), (cb,)), ((), ())), preferred_element_type=F32)


def flip_core(x):
    n = lax.axis_size("ctx")
    return lax.ppermute(x, "ctx", [(i, i ^ 1) for i in range(n)])


def from_chip(x, steps):
    n = lax.axis_size("ctx")
    return lax.ppermute(x, "ctx", [((i + 2 * steps) % n, i) for i in range(n)])


def to_later(x, steps):
    n = lax.axis_size("ctx")
    return lax.ppermute(x, "ctx", [(i, i + 2 * steps) for i in range(n - 2 * steps)])


def to_earlier(x, steps):
    n = lax.axis_size("ctx")
    return lax.ppermute(x, "ctx", [(i + 2 * steps, i) for i in range(n - 2 * steps)])


def swap_dp(x, mask):
    n = lax.axis_size("dp")
    return lax.ppermute(x, "dp", [(i, i ^ mask) for i in range(n)])


def whole_call(kernel, info, args, outs, scratch=(), flops=0, name=None):
    size = sum(math.prod(a.shape) * a.dtype.itemsize for a in args)
    size += sum(math.prod(s) * jnp.dtype(d).itemsize for s, d in outs)
    vmem = pl.BlockSpec(memory_space=pltpu.VMEM)
    return pl.pallas_call(
        kernel,
        in_specs=[pl.BlockSpec(memory_space=pltpu.SMEM)] + [vmem] * len(args),
        out_specs=[vmem] * len(outs),
        out_shape=[jax.ShapeDtypeStruct(s, d) for s, d in outs],
        scratch_shapes=list(scratch),
        cost_estimate=pl.CostEstimate(flops=flops, bytes_accessed=size, transcendentals=0),
        name=name,
    )(info, *args)


def project_kernel(chips, data, info, *refs):
    xs = refs[:data]
    own = refs[data : data + chips]
    other = refs[data + chips]
    weight = refs[data + chips + 1]
    outs = refs[data + chips + 2 :]
    z, k = info[0], info[1]
    rows = own[0].shape[0]
    for s in range(chips):
        base = lax.rem(z + s, chips) * (2 * rows)
        weight[pl.ds(pl.multiple_of(base + k * rows, rows), rows), :] = own[s][...]
        weight[pl.ds(pl.multiple_of(base + (1 - k) * rows, rows), rows), :] = other[s]
    full = jnp.concatenate([x[...] for x in xs], axis=0)
    tokens = xs[0].shape[0]
    cols = weight.shape[1]
    step = min(cols, 256)
    for c in range(0, cols, step):
        part = dot(full, weight[:, c : c + step], 1, 0)
        for i, out in enumerate(outs):
            out[:, c : c + step] = part[i * tokens : (i + 1) * tokens].astype(out.dtype)


def kv_kernel(data, info, *refs):
    parts = refs[:data]
    cos, sin, out = refs[data:]
    for h in range(out.shape[0]):
        key = value = 0.0
        for p in parts:
            key = key + p[:, 2 * h * DH : (2 * h + 1) * DH].astype(F32)
            value = value + p[:, (2 * h + 1) * DH : (2 * h + 2) * DH].astype(F32)
        key = key * cos[...] + pltpu.roll(key, DH // 2, 1) * sin[...]
        out[h, :, :DH] = key.astype(BF16)
        out[h, :, DH:] = value.astype(BF16)


def pair_sum_kernel(info, own, other, *outs):
    for s, out in enumerate(outs):
        out[...] = (own[s].astype(F32) + other[s].astype(F32)).astype(out.dtype)


def grad_projected_kernel(chips, info, *refs):
    parts = refs[:chips]
    cos, sin, out = refs[chips:]
    for h in range(parts[0].shape[0]):
        key = value = 0.0
        for p in parts:
            key = key + p[h, :, :DH].astype(F32)
            value = value + p[h, :, DH:].astype(F32)
        key = key * cos[...] - pltpu.roll(key, DH // 2, 1) * sin[...]
        out[:, 2 * h * DH : (2 * h + 1) * DH] = key.astype(BF16)
        out[:, (2 * h + 1) * DH : (2 * h + 2) * DH] = value.astype(BF16)


def grad_weight_kernel(data, chips, info, *refs):
    xs = refs[:data]
    gs = refs[data : 2 * data]
    own, other, total = refs[2 * data :]
    z, k = info[0], info[1]
    rows = own.shape[1]
    x = jnp.concatenate([r[...] for r in xs], axis=0)
    g = jnp.concatenate([r[...] for r in gs], axis=0)
    total[...] = dot(x, g, 0, 0).astype(BF16)
    for s in range(chips):
        base = lax.rem(z + s, chips) * (2 * rows)
        own[s] = total[pl.ds(pl.multiple_of(base + k * rows, rows), rows), :]
        other[s] = total[pl.ds(pl.multiple_of(base + (1 - k) * rows, rows), rows), :]


def grad_inputs_kernel(data, groups, info, *refs):
    gs = refs[: data * groups]
    ws = refs[data * groups : data * groups + groups]
    outs = refs[data * groups + groups :]
    tokens = outs[0].shape[0]
    acc = None
    for c in range(groups):
        g = jnp.concatenate([gs[c * data + i][...] for i in range(data)], axis=0)
        part = dot(g, ws[c][...], 1, 1)
        acc = part if acc is None else acc + part
    for i, out in enumerate(outs):
        out[...] = acc[i * tokens : (i + 1) * tokens].astype(BF16)


def sum_kernel(info, *refs):
    out = refs[-1]
    total = refs[0][...].astype(F32)
    for r in refs[1:-1]:
        total = total + r[...].astype(F32)
    out[...] = total


def attention_kernel(chips, pairs, scale, info, q_ref, do_ref, *refs):
    own = refs[:chips]
    near, far = refs[chips], refs[chips + 1]
    o_ref, dq_ref, own_out, other_out, kv, kv_t, acc = refs[-7:]
    g = pl.program_id(1)
    z, k = info[0], info[1]
    T = q_ref.shape[0]
    blk = 2 * T
    c = scale * math.log2(math.e)

    @pl.when(g == 0)
    def _():
        for s in range(chips):
            kv[s * blk : s * blk + T, :] = own[s][0]
            kv[s * blk + T : (s + 1) * blk, :] = near[0] if s == 0 else far[s - 1, 0]
        kv_t[...] = kv[...].T
        acc[...] = jnp.zeros_like(acc)

    q2 = jnp.concatenate([q_ref[:, :DH], q_ref[:, DH:]], axis=0)
    d2 = jnp.concatenate([do_ref[:, :DH], do_ref[:, DH:]], axis=0)
    scores = []
    top = None
    for s in range(chips):
        x = dot(kv[s * blk : (s + 1) * blk, :DH], q2, 1, 1)
        if s == 0:
            row = lax.broadcasted_iota(jnp.int32, (blk, blk), 1) % T + k * T
            at = lax.broadcasted_iota(jnp.int32, (blk, blk), 0)
            at = jnp.where(at < T, at + k * T, at - k * T)
            x = jnp.where(at <= row, x, -jnp.inf)
            top = jnp.max(x, axis=0, keepdims=True)
        else:
            here = jnp.max(x, axis=0, keepdims=True)
            top = jnp.maximum(top, jnp.where(s <= z, here, -jnp.inf))
        scores.append(x)
    top = top * c
    out = total = None
    weights = []
    for s in range(chips):
        top_here = top if s == 0 else jnp.where(s <= z, top, jnp.inf)
        w = jnp.exp2(scores[s] * c - top_here)
        part = dot(kv_t[DH:, s * blk : (s + 1) * blk], w.astype(BF16), 1, 0)
        row_sum = jnp.sum(w, axis=0, keepdims=True)
        total = row_sum if total is None else total + row_sum
        out = part if out is None else out + part
        weights.append(w)
    inverse = 1.0 / total
    o_b = (out * inverse).T.astype(BF16)
    o_ref[:, :DH] = o_b[:T]
    o_ref[:, DH:] = o_b[T:]
    inverse_col = jnp.broadcast_to(inverse, (8, blk)).T[:, :1]
    dn = (d2.astype(F32) * inverse_col).astype(BF16)
    delta = jnp.sum(dn.astype(F32) * o_b.astype(F32), axis=1, keepdims=True)
    delta = jnp.broadcast_to(delta, (blk, 128)).T[:1, :]
    dq = None
    for s in range(chips):
        sl = slice(s * blk, (s + 1) * blk)
        dp = dot(kv[sl, DH:], dn, 1, 1)
        ds = (weights[s] * (dp - delta)).astype(BF16)
        part = dot(kv_t[:DH, sl], ds, 1, 0)
        dq = part if dq is None else dq + part
        acc[sl, :DH] += dot(ds, q2, 1, 0)
        acc[sl, DH:] += dot(weights[s].astype(BF16), dn, 1, 0)
    dq = (dq * scale).T.astype(BF16)
    dq_ref[:, :DH] = dq[:T]
    dq_ref[:, DH:] = dq[T:]

    @pl.when(g == pairs - 1)
    def _():
        for s in range(chips):
            for ref, lo in ((own_out, s * blk), (other_out, s * blk + T)):
                ref[s, 0, :, :DH] = (acc[lo : lo + T, :DH] * scale).astype(BF16)
                ref[s, 0, :, DH:] = acc[lo : lo + T, DH:].astype(BF16)


def attention(info, q, do, own, near, far, first_head, kv_heads, carried):
    chips = len(own)
    heads, T = own[0].shape[0], own[0].shape[1]
    q_heads = q.shape[1] // DH
    pairs = q_heads // kv_heads // 2
    keys = chips * 2 * T
    tile = pl.BlockSpec((T, 2 * DH), lambda h, g, i: (0, (first_head + h) * pairs + g))
    one = pl.BlockSpec((1, T, 2 * DH), lambda h, g, i: (h, 0, 0))
    rest = pl.BlockSpec((chips - 1, 1, T, 2 * DH), lambda h, g, i: (0, h, 0, 0))
    every = pl.BlockSpec((chips, 1, T, 2 * DH), lambda h, g, i: (0, h, 0, 0))
    anywhere = pl.BlockSpec(memory_space=pl.ANY)
    grads = jax.ShapeDtypeStruct((chips, heads, T, 2 * DH), BF16)
    rows = heads * pairs * 2 * T
    args = [q, do, *own, near, far, *carried]
    aliases = {1 + len(args) - len(carried) + i: i for i in range(len(carried))}
    return pl.pallas_call(
        functools.partial(attention_kernel, chips, pairs, DH**-0.5),
        grid_spec=pltpu.PrefetchScalarGridSpec(
            num_scalar_prefetch=1,
            grid=(heads, pairs),
            in_specs=[tile, tile] + [one] * (chips + 1) + [rest] + [anywhere] * len(carried),
            out_specs=[tile, tile, every, every],
            scratch_shapes=[
                pltpu.VMEM((keys, 2 * DH), BF16),
                pltpu.VMEM((2 * DH, keys), BF16),
                pltpu.VMEM((keys, 2 * DH), F32),
            ],
        ),
        out_shape=[
            jax.ShapeDtypeStruct(q.shape, BF16),
            jax.ShapeDtypeStruct(q.shape, BF16),
            grads,
            grads,
        ],
        input_output_aliases=aliases,
        cost_estimate=pl.CostEstimate(
            flops=2 * 14 * rows * keys * DH,
            bytes_accessed=8 * rows * DH + 16 * heads * keys * DH,
            transcendentals=rows * keys,
        ),
        name="attention",
    )(info, *args)


def on_device(inputs, queries, grad_output, kv_weight):
    T, width = inputs.shape[1], inputs.shape[2]
    rows, kv_width = kv_weight.shape
    kv_half = kv_width // 2
    kv_heads = kv_half // DH
    data = lax.axis_size("dp")
    chips = lax.axis_size("ctx") // 2
    d = lax.axis_index("dp")
    c = lax.axis_index("ctx")
    info = jnp.stack([c // 2, c % 2]).astype(jnp.int32)
    part_width = width // data
    per = kv_heads // CHUNKS
    cols = per * 2 * DH

    def head_cols(h):
        return [kv_weight[:, h * DH : (h + 1) * DH], kv_weight[:, kv_half + h * DH : kv_half + (h + 1) * DH]]

    own_w = []
    for i in range(CHUNKS):
        w = jnp.concatenate(sum([head_cols(i * per + h) for h in range(per)], []), axis=1)
        own_w.append([w] + [from_chip(w, s) for s in range(1, chips)])
    x = inputs[0]
    xs = []
    for m in range(data):
        piece = lax.dynamic_slice_in_dim(x, (d ^ m) * part_width, part_width, 1)
        xs.append(piece if m == 0 else swap_dp(piece, m))

    positions = (c * T + jnp.arange(T, dtype=jnp.int32)).astype(F32)
    frequency = ROPE_BASE ** (-2.0 * jnp.arange(DH // 2, dtype=F32) / DH)
    angles = positions[:, None] * frequency[None, :]
    cos = jnp.concatenate([jnp.cos(angles)] * 2, axis=1)
    sin = jnp.sin(angles)
    sin = jnp.concatenate([-sin, sin], axis=1)

    weights = []
    kv = []
    for i in range(CHUNKS):
        other_w = flip_core(jnp.stack(own_w[i]))
        weight, *parts = whole_call(
            functools.partial(project_kernel, chips, data),
            info,
            [*xs, *own_w[i], other_w],
            [((part_width, cols), BF16), ((T, cols), F32)] + [((T, cols), BF16)] * (data - 1),
            flops=2 * data * T * part_width * cols,
            name="project",
        )
        weights.append(weight)
        parts = [parts[0]] + [swap_dp(parts[m], m) for m in range(1, data)]
        (block,) = whole_call(
            functools.partial(kv_kernel, data), info, [*parts, cos, sin], [((per, T, 2 * DH), BF16)], name="kv"
        )
        own = [block] + [to_later(block, s) for s in range(1, chips)]
        near = flip_core(block)
        far = flip_core(jnp.stack(own[1:]))
        kv.append((own, near, far))

    carried = []
    all_grads = []
    grad_weight = []
    for i in range(CHUNKS):
        own, near, far = kv[i]
        *carried, own_g, other_g = attention(
            info, queries[0], grad_output[0], own, near, far, i * per, kv_heads, carried
        )
        shape = (per, T, 2 * DH)
        sums = whole_call(
            pair_sum_kernel,
            info,
            [own_g, flip_core(other_g)],
            [(shape, F32)] + [(shape, BF16)] * (chips - 1),
            name="pair_sum",
        )
        sums = [sums[0]] + [to_earlier(sums[s], s) for s in range(1, chips)]
        (grad,) = whole_call(
            functools.partial(grad_projected_kernel, chips), info, [*sums, cos, sin], [((T, cols), BF16)], name="grad_kv"
        )
        grads = [grad] + [swap_dp(grad, m) for m in range(1, data)]
        all_grads += grads
        gw_shape = (chips, rows, cols)
        gw_own, gw_other = whole_call(
            functools.partial(grad_weight_kernel, data, chips),
            info,
            [*xs, *grads],
            [(gw_shape, BF16)] * 2,
            scratch=[pltpu.VMEM((part_width, cols), BF16)],
            flops=2 * data * T * part_width * cols,
            name="grad_weight",
        )
        sums = whole_call(
            pair_sum_kernel,
            info,
            [gw_own, flip_core(gw_other)],
            [((rows, cols), F32)] + [((rows, cols), BF16)] * (chips - 1),
            name="pair_sum_w",
        )
        sums = [sums[0]] + [from_chip(sums[s], chips - s) for s in range(1, chips)]
        (total,) = whole_call(sum_kernel, info, sums, [((rows, cols), F32)], name="sum_w")
        grad_weight.append(total)

    pieces = whole_call(
        functools.partial(grad_inputs_kernel, data, CHUNKS),
        info,
        [*all_grads, *weights],
        [((T, part_width), BF16)] * data,
        flops=2 * data * T * part_width * kv_width,
        name="grad_inputs",
    )
    grad_inputs = jnp.zeros((T, width), BF16)
    for m in range(data):
        piece = pieces[m] if m == 0 else swap_dp(pieces[m], m)
        grad_inputs = lax.dynamic_update_slice_in_dim(grad_inputs, piece, (d ^ m) * part_width, 1)

    gw = jnp.concatenate(grad_weight, axis=1).reshape(rows, kv_heads, 2, DH)
    gw = gw.transpose(0, 2, 1, 3).reshape(rows, kv_width)
    attn_out, grad_query = carried
    return attn_out[None], grad_query[None], grad_inputs[None], gw


def solution(mesh):
    token = P("dp", "ctx", None)
    weight = P(("dp", "ctx"), None)
    return jax.shard_map(
        on_device,
        mesh=mesh,
        in_specs=(token, token, token, weight),
        out_specs=(token, token, token, weight),
        check_vma=False,
    )
```
